32 devices in a mesh: groups: 2 (over y), px: 16 (over z, x, core).
Axes of the slice: x: 2, y: 2, z: 4, core: 2. Of those that a mesh axis runs over, the one named last changes fastest.
Arguments:
- features: bfloat16 [32, 256, 256, 256], P(None, ('groups', 'px')), parts along dimension 1, may hold values from -6 to 6
- pointwise_weight: bfloat16 [32, 32], replicated, may hold values from -1 to 1
- pointwise_bias: float32 [32], replicated, may hold values from -3 to 3
- spectral_weight: float32 [2, 32, 32, 16384], P(None, None, None, 'px'), may hold values from -6 to 6
Outputs:
- updated: bfloat16 [32, 256, 256, 256], P(None, ('groups', 'px')), parts along dimension 1
The draws below stay inside these ranges and needn't reach their ends.
There are 2 independent parts, one for each index of `groups`. The reference program is written for one: setup_inputs(seed, part) draws one part's arguments, and reference() takes and returns one part's arrays. A program takes and returns all parts, laid end to end along the dimension named above; an argument that names none is the same for every part. Nothing has to cross between parts.
All inputs are finite; a program needn't handle non-finite values.
Results may differ from the reference program's by a relative error of at most 0.0025.
Values sent between devices are 32-bit elements; how exact they have to be, the bound alone decides.
A program may use at most 256 MiB of HBM per device.

```python
import math
import jax
import jax.numpy as jnp
from jax import lax

C = 32
X = 128
Y = 256
Z = 256
KX = 32
KY = 32
KZ = 16
MODES = 16384


def steps_of(key, shape, cuts, least, largest):
    level = 1.0
    for axis_at, parts in cuts:
        draws = jax.random.uniform(jax.random.fold_in(jax.random.fold_in(key, 6), axis_at), (parts,), jnp.float32, least / len(cuts), largest / len(cuts))
        level = level * jnp.repeat(jnp.exp(draws), shape[axis_at] // parts).reshape((-1,) + (1,) * (len(shape) - 1 - axis_at))
    return level


def gaussian(key, dims, scale, most, cuts=(), kind=jnp.bfloat16):
    drawn = scale * jax.random.normal(key, dims, jnp.float32)
    if cuts:
        drawn = drawn * steps_of(key, dims, cuts, -0.22, 0.18)
    return jnp.clip(drawn, -most, most).astype(kind)


def setup_inputs(seed: int = 0, part: int = 0) -> dict:
    seeds = jax.random.split(jax.random.key(seed), 5)
    own_keys = jax.random.split(jax.random.fold_in(seeds[4], part), 5)
    features = gaussian(own_keys[0], (C, X, Y, Z), 1.0, 6.0, ((1, 16),))
    pointwise_weight = gaussian(seeds[1], (C, C), C ** -0.5, 1.0)
    pointwise_bias = gaussian(seeds[2], (C,), 0.5, 3.0, (), jnp.float32)
    spectral_weight = gaussian(seeds[3], (2, C, C, MODES), 1.0, 6.0, ((3, 16),), jnp.float32)
    return {"features": features, "pointwise_weight": pointwise_weight, "pointwise_bias": pointwise_bias, "spectral_weight": spectral_weight}


TWO_PI = 2.0 * math.pi


def signed_modes(number):
    ladder = jnp.arange(number, dtype=jnp.int32)
    return jnp.where(ladder < number // 2, ladder, ladder - number)


def phase_table(positions, frequency, length):
    product = (positions[:, None] * frequency[None, :]) % length
    return product.astype(jnp.float32) * (TWO_PI / length)


def forward_table(positions):
    x_phase = phase_table(positions, signed_modes(KX), X)
    cosine = jnp.cos(x_phase)
    sine = jnp.sin(x_phase)
    return jnp.stack([jnp.stack([cosine, -sine], axis=1), jnp.stack([sine, cosine], axis=1)], axis=0)


def inverse_table(positions):
    x_phase = phase_table(positions, signed_modes(KX), X)
    cosine = jnp.cos(x_phase)
    sine = jnp.sin(x_phase)
    return jnp.stack([jnp.stack([cosine, sine], axis=1), jnp.stack([-sine, cosine], axis=1)], axis=0)


def spectra_local(features):
    channels = features.shape[0]
    planes = features.shape[1]
    z_phase = phase_table(jnp.arange(Z, dtype=jnp.int32), jnp.arange(KZ, dtype=jnp.int32), Z)
    z_table = jnp.concatenate([jnp.cos(z_phase), -jnp.sin(z_phase)], axis=1).astype(jnp.bfloat16)
    flat = features.reshape(channels * planes * Y, Z)
    along_z = jnp.dot(flat, z_table, preferred_element_type=jnp.float32)
    stacked = along_z.reshape(channels, planes, Y, 2, KZ).transpose(3, 0, 1, 4, 2)
    y_phase = phase_table(jnp.arange(Y, dtype=jnp.int32), signed_modes(KY), Y)
    cosine = jnp.einsum('rcxky,yj->rcxjk', stacked, jnp.cos(y_phase), precision=lax.Precision.HIGHEST)
    sine = jnp.einsum('rcxky,yj->rcxjk', stacked, jnp.sin(y_phase), precision=lax.Precision.HIGHEST)
    real_part = cosine[0] + sine[1]
    imag_part = cosine[1] - sine[0]
    return jnp.stack([real_part, imag_part]).reshape(2, channels, planes, KY * KZ)


def along_first(partial_value, table):
    return jnp.einsum('rcxq,rxsk->qsck', partial_value, table, precision=lax.Precision.HIGHEST)


def contract(left, right):
    return jnp.einsum('im,iom->om', left, right, precision=lax.Precision.HIGHEST)


def mix_modes(spectrum, weights):
    real_part = contract(spectrum[0], weights[0]) - contract(spectrum[1], weights[1])
    imag_part = contract(spectrum[0], weights[1]) + contract(spectrum[1], weights[0])
    return jnp.stack([real_part, imag_part])


def back_first(blended, table):
    return jnp.einsum('rcqk,rxsk->scxq', blended, table, precision=lax.Precision.HIGHEST)


def finish_planes(spread, features, pointwise_weight, pointwise_bias):
    channels = features.shape[0]
    planes = features.shape[1]
    folded = spread.reshape(2, channels, planes, KY, KZ)
    y_phase = phase_table(jnp.arange(Y, dtype=jnp.int32), signed_modes(KY), Y)
    cosine = jnp.einsum('rcxjk,yj->rcxky', folded, jnp.cos(y_phase), precision=lax.Precision.HIGHEST)
    sine = jnp.einsum('rcxjk,yj->rcxky', folded, jnp.sin(y_phase), precision=lax.Precision.HIGHEST)
    halves = jnp.concatenate([cosine[0] - sine[1], sine[0] + cosine[1]], axis=2)
    z_phase = phase_table(jnp.arange(Z, dtype=jnp.int32), jnp.arange(KZ, dtype=jnp.int32), Z)
    factor = jnp.where(jnp.arange(KZ, dtype=jnp.int32) == 0, 1.0, 2.0).astype(jnp.float32) / (1.0 * X * Y * Z)
    z_table = jnp.concatenate([factor[:, None] * jnp.cos(z_phase).T, -factor[:, None] * jnp.sin(z_phase).T], axis=0)
    spectral = jnp.einsum('cxjy,jz->cxyz', halves, z_table, precision=lax.Precision.HIGHEST)
    linear = jnp.dot(pointwise_weight, features.reshape(channels, planes * Y * Z), preferred_element_type=jnp.float32).reshape(channels, planes, Y, Z)
    summed = spectral + linear + pointwise_bias[:, None, None, None]
    inner = 0.7978845608 * (summed + 0.044715 * summed * summed * summed)
    return (0.5 * summed * (1.0 + jnp.tanh(inner))).astype(jnp.bfloat16)


def reference(features, pointwise_weight, pointwise_bias, spectral_weight):
    indices = jnp.arange(X, dtype=jnp.int32)

    def forward_plane(plane_index):
        return spectra_local(lax.dynamic_slice_in_dim(features, plane_index, 1, 1))[:, :, 0, :]

    partial_value = jnp.moveaxis(lax.map(forward_plane, indices), 0, 2)
    spectrum = along_first(partial_value, forward_table(indices)).transpose(1, 2, 0, 3).reshape(2, C, KY * KZ * KX)
    blended = mix_modes(spectrum, spectral_weight).reshape(2, C, KY * KZ, KX)
    spread = back_first(blended, inverse_table(indices))

    def finish_plane(plane_index):
        return finish_planes(lax.dynamic_slice_in_dim(spread, plane_index, 1, 2), lax.dynamic_slice_in_dim(features, plane_index, 1, 1), pointwise_weight, pointwise_bias)[:, 0]

    return jnp.moveaxis(lax.map(finish_plane, indices), 0, 1)
```

```python
import functools
import math

import jax
import jax.numpy as jnp
import numpy as np
from jax import lax
from jax.experimental import pallas as pl
from jax.experimental.pallas import tpu as pltpu
from jax.sharding import PartitionSpec as P

KX = 32
KY = 32
KZ = 16
LANES = 128
PACK = LANES // KZ
ROWS = 16

TWO_PI = 2.0 * math.pi


def signed_modes(number):
    ladder = np.arange(number)
    return np.where(ladder < number // 2, ladder, ladder - number)


def phase_table(length, frequency):
    product = np.arange(length)[:, None] * frequency[None, :] % length
    return product.astype(np.float32) * np.float32(TWO_PI / length)


def rounded(table):
    return np.asarray(table).astype(jnp.bfloat16)


def split(table):
    high = rounded(table)
    return high, rounded(table - high.astype(np.float32))


def forward_table(length):
    phase = phase_table(length, signed_modes(KX))
    cosine, sine = np.cos(phase), np.sin(phase)
    return np.stack([np.stack([cosine, -sine], axis=1), np.stack([sine, cosine], axis=1)], axis=0)


def inverse_table(length):
    phase = phase_table(length, signed_modes(KX))
    cosine, sine = np.cos(phase), np.sin(phase)
    return np.stack([np.stack([cosine, sine], axis=1), np.stack([-sine, cosine], axis=1)], axis=0)


def packed_z_table(depth):
    phase = phase_table(depth, np.arange(KZ))
    table = np.zeros((PACK, depth, 2, PACK, KZ), np.float32)
    for c in range(PACK):
        table[c, :, 0, c] = np.cos(phase)
        table[c, :, 1, c] = -np.sin(phase)
    return rounded(table.reshape(PACK * depth, 2 * LANES))


def forward_kernel(f_ref, z_ref, y_ref, out_ref):
    groups = f_ref.shape[0] // PACK
    for g in range(groups):
        wide = jnp.concatenate([f_ref[g * PACK + c, 0] for c in range(PACK)], axis=1)
        along = jnp.dot(wide, z_ref[...], preferred_element_type=jnp.float32)
        high = along.astype(jnp.bfloat16)
        low = (along - high.astype(jnp.float32)).astype(jnp.bfloat16)
        both = jnp.dot(y_ref[...], high, preferred_element_type=jnp.float32)
        rest = jnp.dot(y_ref[: 2 * KY], low, preferred_element_type=jnp.float32)
        total = both[: 2 * KY] + both[2 * KY :] + rest
        cosine, sine = total[:KY], total[KY:]
        out_ref[:, 0, g, :] = cosine[:, :LANES] + sine[:, LANES:]
        out_ref[:, 0, groups + g, :] = cosine[:, LANES:] - sine[:, :LANES]


def spectra_local(features):
    channels, planes, height, depth = features.shape
    groups = channels // PACK
    y_phase = phase_table(height, signed_modes(KY)).T
    high, low = split(np.concatenate([np.cos(y_phase), np.sin(y_phase)], axis=0))
    return pl.pallas_call(
        forward_kernel,
        grid=(planes,),
        out_shape=jax.ShapeDtypeStruct((KY, planes, 2 * groups, LANES), jnp.float32),
        in_specs=[
            pl.BlockSpec((channels, 1, height, depth), lambda x: (0, x, 0, 0)),
            pl.BlockSpec((PACK * depth, 2 * LANES), lambda x: (0, 0)),
            pl.BlockSpec((4 * KY, height), lambda x: (0, 0)),
        ],
        out_specs=pl.BlockSpec((KY, 1, 2 * groups, LANES), lambda x: (0, x, 0, 0)),
        compiler_params=pltpu.CompilerParams(vmem_limit_bytes=48 << 20),
        name="forward_planes",
    )(features, jnp.asarray(packed_z_table(depth)), jnp.asarray(np.concatenate([high, low], axis=0)))


def contract(left, right):
    return jnp.einsum("im,iom->om", left, right, precision=lax.Precision.HIGHEST)


def mix_modes(spectrum, weights):
    real_part = contract(spectrum[0], weights[0]) - contract(spectrum[1], weights[1])
    imag_part = contract(spectrum[0], weights[1]) + contract(spectrum[1], weights[0])
    return jnp.stack([real_part, imag_part])


def inverse_kernel(f_ref, q_ref, place_ref, y_ref, z_ref, mix_ref, bias_ref, out_ref, held):
    channels, _, height, depth = f_ref.shape
    lane = lax.broadcasted_iota(jnp.int32, (height, LANES), 1)

    def along_y(c, carry):
        modes = q_ref[0, c]
        high = modes.astype(jnp.bfloat16)
        low = (modes - high.astype(jnp.float32)).astype(jnp.bfloat16)
        both = jnp.concatenate([high, low], axis=0)
        placed = jnp.dot(both, place_ref[...], preferred_element_type=jnp.float32)
        placed = placed.astype(jnp.bfloat16)
        high = jnp.concatenate([placed[:KY, :LANES], placed[:KY, LANES:]], axis=0)
        low = jnp.concatenate([placed[KY:, :LANES], placed[KY:, LANES:]], axis=0)
        stack = jnp.concatenate([high, high, low], axis=0)
        value = jnp.dot(y_ref[...], stack, preferred_element_type=jnp.float32)
        top = value.astype(jnp.bfloat16).astype(jnp.float32)
        part = jnp.where((lane >= 2 * KZ) & (lane < 4 * KZ), value - top, top)
        held[c] = jnp.where(lane < 6 * KZ, part, bias_ref[c]).astype(jnp.bfloat16)
        return carry

    lax.fori_loop(0, channels, along_y, 0, unroll=4)

    def finish(t, carry):
        rows = pl.ds(pl.multiple_of(t * ROWS, ROWS), ROWS)
        local = f_ref[:, 0, rows, :].reshape(channels * ROWS, depth)
        waves = held[:, rows, :].reshape(channels * ROWS, LANES)
        summed = jnp.dot(mix_ref[...], local, preferred_element_type=jnp.float32)
        summed = summed + jnp.dot(waves, z_ref[...], preferred_element_type=jnp.float32)
        inner = summed * (0.7978845608 + (0.7978845608 * 0.044715) * (summed * summed))
        half = 0.5 * summed
        result = (half + half * jnp.tanh(inner)).astype(jnp.bfloat16)
        out_ref[:, 0, rows, :] = result.reshape(channels, ROWS, depth)
        return carry

    lax.fori_loop(0, height // ROWS, finish, 0)


def finish_planes(modes, features, pointwise_weight, pointwise_bias, cells):
    channels, planes, height, depth = features.shape
    y_phase = phase_table(height, signed_modes(KY))
    high, low = split(np.concatenate([np.cos(y_phase), np.sin(y_phase)], axis=1))
    y_table = np.concatenate([high, low, high], axis=1)
    z_phase = phase_table(depth, np.arange(KZ)).T
    factor = (np.where(np.arange(KZ) == 0, 1.0, 2.0) / cells).astype(np.float32)[:, None]
    high, low = split(np.concatenate([factor * np.cos(z_phase), -factor * np.sin(z_phase)], axis=0))
    ones = np.zeros((2 * KZ, depth), np.float32)
    ones[:3] = 1.0
    z_table = np.concatenate([high, high, low, rounded(ones)], axis=0)
    mix = pointwise_weight[:, None, :, None] * jnp.eye(ROWS, dtype=jnp.bfloat16)[None, :, None, :]
    mix = mix.reshape(channels * ROWS, channels * ROWS)
    first = lax.reduce_precision(pointwise_bias, 8, 7)
    second = lax.reduce_precision(pointwise_bias - first, 8, 7)
    third = pointwise_bias - first - second
    bias = jnp.stack([first, second, third], axis=1)
    bias = jnp.pad(bias, ((0, 0), (6 * KZ, LANES - 6 * KZ - 3)))[:, None, :]
    same = np.eye(2 * KZ, dtype=np.float32)
    turned = np.roll(same, KZ, axis=1) * np.where(np.arange(2 * KZ) < KZ, -1.0, 1.0)
    repeats = LANES // (2 * KZ)
    place = np.concatenate([np.tile(same, (1, repeats)), np.tile(turned, (1, repeats))], axis=1)
    plane = pl.BlockSpec((channels, 1, height, depth), lambda x: (0, x, 0, 0))
    return pl.pallas_call(
        inverse_kernel,
        grid=(planes,),
        out_shape=jax.ShapeDtypeStruct(features.shape, jnp.bfloat16),
        in_specs=[
            plane,
            pl.BlockSpec((1, channels, KY, 2 * KZ), lambda x: (x, 0, 0, 0)),
            pl.BlockSpec((2 * KZ, 2 * LANES), lambda x: (0, 0)),
            pl.BlockSpec((height, 6 * KY), lambda x: (0, 0)),
            pl.BlockSpec((LANES, depth), lambda x: (0, 0)),
            pl.BlockSpec((channels * ROWS, channels * ROWS), lambda x: (0, 0)),
            pl.BlockSpec((channels, 1, LANES), lambda x: (0, 0, 0)),
        ],
        out_specs=plane,
        scratch_shapes=[pltpu.VMEM((channels, height, LANES), jnp.bfloat16)],
        compiler_params=pltpu.CompilerParams(vmem_limit_bytes=56 << 20),
        name="inverse_planes",
    )(features, modes, jnp.asarray(rounded(place)), jnp.asarray(y_table), jnp.asarray(z_table), mix, bias)


def on_device(parts, features, pointwise_weight, pointwise_bias, spectral_weight):
    channels, planes, height, depth = features.shape
    groups = channels // PACK
    length = planes * parts
    held_y = max(KY // parts, 1)
    cuts = parts * held_y // KY
    held_z = KZ // cuts
    exact = functools.partial(jnp.einsum, precision=lax.Precision.HIGHEST)

    sent = spectra_local(features)
    if cuts > 1:
        sent = sent.reshape(KY, planes, 2 * channels, cuts, held_z).transpose(0, 3, 1, 2, 4)
    sent = sent.reshape(parts, held_y * planes * 2 * channels * held_z // LANES, LANES)
    gathered = lax.all_to_all(sent, "px", split_axis=0, concat_axis=0, tiled=True)
    gathered = gathered.reshape(parts, held_y, planes, 2, channels, held_z)
    table = jnp.asarray(forward_table(length).reshape(2, parts, planes, 2, KX))
    spectrum = exact("sjprck,rsptm->tcjkm", gathered, table)
    blended = mix_modes(spectrum.reshape(2, channels, held_y * held_z * KX), spectral_weight)
    blended = blended.reshape(2, channels, held_y, held_z, KX)
    table = jnp.asarray(inverse_table(length).reshape(2, parts, planes, 2, KX))
    sent = exact("rcjkm,rsptm->spjtck", blended, table)
    sent = sent.reshape(parts, held_y * planes * 2 * channels * held_z // LANES, LANES)
    spread = lax.all_to_all(sent, "px", split_axis=0, concat_axis=0, tiled=True)
    spread = spread.reshape(KY // held_y, cuts, planes, held_y, 2, channels, held_z)
    modes = spread.transpose(2, 5, 0, 3, 4, 1, 6).reshape(planes, channels, KY, 2 * KZ)
    return finish_planes(
        modes, features, pointwise_weight, pointwise_bias, 1.0 * length * height * depth
    )


def solution(mesh):
    in_specs = (P(None, ("groups", "px"), None, None), P(), P(), P(None, None, None, "px"))
    out_specs = P(None, ("groups", "px"), None, None)
    return jax.shard_map(
        functools.partial(on_device, mesh.shape["px"]),
        mesh=mesh,
        in_specs=in_specs,
        out_specs=out_specs,
        check_vma=False,
    )
```
